32 devices in a mesh: strip: 8 (over z, x), freq: 4 (over y, core).
Axes of the slice: x: 2, y: 2, z: 4, core: 2. Of those that a mesh axis runs over, the one named last changes fastest.
Arguments:
- fields: bfloat16 [3, 4, 16, 1536, 1536], P(None, None, 'freq', 'strip'), may hold values from -6 to 6
- step_index: int32 [16], replicated, may hold values from 0 to 75, as said below
- omegas: float32 [4], replicated, may hold values from 0.05 to 0.5
- col_phase: bfloat16 [4, 3, 2, 1536, 512], P('freq', None, None, 'strip'), may hold values from -0.109375 to 0.109375
- row_phase: bfloat16 [4, 3, 2, 1536, 512], P('freq', None, None, 'strip'), may hold values from -0.09375 to 0.09375
Outputs:
- far_field: float32 [512, 4, 2, 4, 512], P('strip', 'freq')
The draws below stay inside these ranges and needn't reach their ends.
Inputs may be any that keep to these rules, and one draw needn't show every extreme that they name: `step_index`: strictly increasing, first value 0, last value 5 * 15, consecutive values differ by 2 to 8.
All inputs are finite; a program needn't handle non-finite values.
Results may differ from the reference program's by a relative error of at most 0.0041.
Values may be sent and summed in bfloat16 or wider, within the bound.
A program may use at most 256 MiB of HBM per device.

```python
import math
import jax
import jax.numpy as jnp
from jax import lax

F = 1536
U = 512
V = 512
NF = 4
COMP = 4
FACES = 3
STEPS = 16


def draw_step_index(key, part):
    paired = (STEPS - 2) // 2
    first_gap = jax.random.randint(key, (paired,), 2, 9)
    gaps = jnp.stack([first_gap, 10 - first_gap], 1).reshape(-1)
    gaps = jnp.concatenate([gaps, jnp.full((1,), 5, jnp.int32)])
    values = jnp.concatenate([jnp.zeros((1,), jnp.int32), jnp.cumsum(gaps).astype(jnp.int32)])
    return values.astype(jnp.int32)


def spiked(values, own_key, source, target, blocks, factor):
    owner, partner = [(jnp.arange(values.shape[position]) // (values.shape[position] // blocks)).reshape([-1 if axis == position else 1 for axis in range(values.ndim)]) for position in (source, target)]
    chosen = jax.random.permutation(own_key, blocks)[partner]
    strong = (owner == chosen) | (owner == (partner + blocks // 2) % blocks)
    return jnp.where(strong, factor * values, values)


def levels(own_key, shape, shards, smallest, high):
    def one(axis_at, shards_of):
        steps = jax.random.uniform(jax.random.fold_in(jax.random.fold_in(own_key, 6), axis_at), (shards_of,), jnp.float32, smallest / len(shards), high / len(shards))
        return jnp.repeat(jnp.exp(steps), shape[axis_at] // shards_of).reshape((-1,) + (1,) * (len(shape) - axis_at - 1))

    loudness = one(*shards[0])
    for cut in shards[1:]:
        loudness = loudness * one(*cut)
    return loudness


def noise(key, shape, scale, limit, cuts=(), kind=jnp.bfloat16):
    loudness = levels(key, shape, cuts, -0.22, 0.18) if cuts else 1.0
    entries = jax.random.normal(key, shape, jnp.float32) * scale * loudness
    return jnp.minimum(jnp.maximum(entries, -limit), limit).astype(kind)


def noise_with(own_key, extent, deviation, most, split, heavy, kind=jnp.bfloat16):
    values = deviation * jax.random.normal(own_key, extent, jnp.float32)
    if split:
        values = values * levels(own_key, extent, split, -0.22, 0.18)
    return jnp.clip(spiked(values, jax.random.fold_in(own_key, 3), *heavy), -most, most).astype(kind)


def setup_inputs(seed: int = 0) -> dict:
    arg_keys = jax.random.split(jax.random.key(seed), 6)
    return {
        "fields": noise(arg_keys[0], (FACES, COMP, STEPS, F, F), 1.0, 6.0, ((2, 4), (3, 8))),
        "step_index": draw_step_index(jax.random.fold_in(arg_keys[5], 71), 0),
        "omegas": jnp.clip(jnp.exp(jax.random.uniform(arg_keys[2], (NF,), jnp.float32, math.log(0.05), math.log(0.5))), 0.05, 0.5),
        "col_phase": noise(arg_keys[3], (NF, FACES, 2, F, V), (2 * F) ** -0.5, 0.109375, ((0, 4), (3, 8))),
        "row_phase": noise_with(arg_keys[4], (NF, FACES, 2, F, U), (2 * F * FACES) ** -0.5, 0.09375, ((0, 4), (3, 8)), (3, 4, 8, 2.0)),
    }


def mixed(left, right, form):
    return jnp.einsum(form, left.astype(jnp.float32), right.astype(jnp.float32))


def reference(fields, step_index, omegas, col_phase, row_phase):
    phase = omegas[:, None] * step_index.astype(jnp.float32)[None, :]
    cosine = jnp.cos(phase)
    sine_neg = -jnp.sin(phase)

    def one_freq(which):
        real_sum = jnp.zeros((FACES, COMP, F, F), jnp.float32)
        imag_sum = jnp.zeros((FACES, COMP, F, F), jnp.float32)
        for step in range(STEPS):
            record = fields[:, :, step].astype(jnp.float32)
            real_sum = real_sum + cosine[which, step] * record
            imag_sum = imag_sum + sine_neg[which, step] * record
        spec_real = real_sum.astype(jnp.bfloat16)
        spec_imag = imag_sum.astype(jnp.bfloat16)
        columns = col_phase[which]
        q_real = columns[:, 0]
        q_imag = columns[:, 1]
        form = "scab,sbv->scav"
        image_real = (mixed(spec_real, q_real, form) - mixed(spec_imag, q_imag, form)).astype(jnp.bfloat16)
        image_imag = (mixed(spec_real, q_imag, form) + mixed(spec_imag, q_real, form)).astype(jnp.bfloat16)
        rows_all = row_phase[which]
        p_real = rows_all[:, 0]
        p_imag = rows_all[:, 1]
        form_two = "sau,scav->cuv"
        out_real = mixed(p_real, image_real, form_two) - mixed(p_imag, image_imag, form_two)
        out_imag = mixed(p_real, image_imag, form_two) + mixed(p_imag, image_real, form_two)
        return jnp.stack([out_real, out_imag], 0)

    result = lax.map(one_freq, jnp.arange(NF, dtype=jnp.int32))
    return jnp.transpose(result, (3, 0, 1, 2, 4))
```

```python
import jax
import jax.numpy as jnp
from jax import lax
from jax.sharding import PartitionSpec as P


def partial_sum(weights, own, mate):
    cosine, sine_neg = weights
    steps = own.shape[1]
    records = [own[:, t] for t in range(steps)] + [mate[:, t] for t in range(steps)]
    real = imag = None
    for k, record in enumerate(records):
        record = record.astype(jnp.float32)
        real = cosine[k] * record if real is None else real + cosine[k] * record
        imag = sine_neg[k] * record if imag is None else imag + sine_neg[k] * record
    return real, imag


def on_device(fields, step_index, omegas, col_phase, row_phase):
    n = lax.axis_size("freq")
    strips = lax.axis_size("strip")
    me = lax.axis_index("freq")
    faces, comps, steps = fields.shape[:3]
    freq_local, rows, angles = col_phase.shape[0], row_phase.shape[3], row_phase.shape[4]
    mate_id = me + 1 - 2 * lax.rem(me, 2)
    swap = [(i, i ^ 1) for i in range(n)]
    columns = lax.all_gather(col_phase, "strip", axis=3, tiled=True)

    indices = jnp.concatenate(
        [
            lax.dynamic_slice_in_dim(step_index, me * steps, steps),
            lax.dynamic_slice_in_dim(step_index, mate_id * steps, steps),
        ]
    ).astype(jnp.float32)

    def weights(device, g):
        omega = lax.dynamic_index_in_dim(omegas, device * freq_local + g, keepdims=False)
        phase = omega * indices
        return jnp.cos(phase), -jnp.sin(phase)

    own = [fields[:, c] for c in range(comps)]
    mate = [lax.ppermute(own[c], "freq", swap) for c in range(comps)]
    got = {}
    for c in range(comps):
        for g in range(freq_local):
            for d in range(2, n, 2):
                send = [(i, (i + d) % n) for i in range(n)]
                real, imag = partial_sum(weights(lax.rem(me + d, n), g), own[c], mate[c])
                part = jnp.stack([real.astype(jnp.bfloat16), imag.astype(jnp.bfloat16)])
                got[c, g, d] = lax.ppermute(part, "freq", send)

    def turned(g):
        p_real = row_phase[g, :, 0].reshape(faces, rows, strips, angles // strips)
        p_imag = row_phase[g, :, 1].reshape(faces, rows, strips, angles // strips)
        from_real = jnp.stack([p_real, p_imag], 3)
        from_imag = jnp.stack([-p_imag, p_real], 3)
        both = jnp.stack([from_real, from_imag], 1)
        return both.reshape(faces * 2 * rows, 2 * angles)

    outs = []
    turned_rows = [turned(g) for g in range(freq_local)]
    for c in range(comps):
        per_freq = []
        for g in range(freq_local):
            real, imag = partial_sum(weights(me, g), own[c], mate[c])
            for d in range(2, n, 2):
                real = real + got[c, g, d][0].astype(jnp.float32)
                imag = imag + got[c, g, d][1].astype(jnp.float32)
            s_real = real.astype(jnp.bfloat16)
            s_imag = imag.astype(jnp.bfloat16)
            q_real, q_imag = columns[g, :, 0], columns[g, :, 1]

            def dot(left, right):
                return jnp.einsum("sab,sbv->sav", left, right, preferred_element_type=jnp.float32)

            image_real = (dot(s_real, q_real) - dot(s_imag, q_imag)).astype(jnp.bfloat16)
            image_imag = (dot(s_real, q_imag) + dot(s_imag, q_real)).astype(jnp.bfloat16)
            image = jnp.stack([image_real, image_imag], 1).reshape(faces * 2 * rows, -1)
            far = jnp.einsum("ku,kv->uv", turned_rows[g], image, preferred_element_type=jnp.float32)
            far = lax.psum_scatter(far, "strip", scatter_dimension=0, tiled=True)
            per_freq.append(far.reshape(2, angles // strips, -1).transpose(1, 0, 2))
        outs.append(jnp.stack(per_freq, 1))
    return jnp.stack(outs, 3)


def solution(mesh):
    placed = (
        P(None, None, "freq", "strip", None),
        P(),
        P(),
        P("freq", None, None, "strip", None),
        P("freq", None, None, "strip", None),
    )
    return jax.shard_map(
        on_device,
        mesh=mesh,
        in_specs=placed,
        out_specs=P("strip", "freq", None, None, None),
        check_vma=False,
    )
```

```python
import functools

import jax
import jax.numpy as jnp
from jax import lax
from jax.experimental import pallas as pl
from jax.experimental.pallas import tpu as pltpu
from jax.sharding import PartitionSpec as P


def row_tile(rows, want):
    return want if rows % want == 0 else rows


def time_sums_kernel(sets, w_ref, own_ref, mate_ref, part_ref, mine_ref):
    steps, rows, width = own_ref.shape[2:]
    sub = row_tile(rows, 16)
    lane = row_tile(width, 256)

    def body(i, carry):
        r = pl.ds(pl.multiple_of(i * sub, sub), sub)
        for l in range(width // lane):
            cols = pl.ds(l * lane, lane)
            sums = [None] * (2 * sets)
            for t in range(2 * steps):
                raw = own_ref[0, 0, t, r, cols] if t < steps else mate_ref[0, t - steps, r, cols]
                record = raw.astype(jnp.float32)
                for k in range(2 * sets):
                    term = w_ref[k, t] * record
                    sums[k] = term if t == 0 else sums[k] + term
            for k in range(2 * (sets - 1)):
                part_ref[k // 2, 0, k % 2, r, cols] = sums[k].astype(jnp.bfloat16)
            for k in range(2):
                mine_ref[0, k, r, cols] = sums[2 * (sets - 1) + k]
        return carry

    lax.fori_loop(0, rows // sub, body, 0)


def time_sums(weights, fields, mate, c, first, count):
    steps, rows, width = fields.shape[2:]
    sets = weights.shape[0] // 2
    tile = row_tile(rows, 96)
    return pl.pallas_call(
        functools.partial(time_sums_kernel, sets),
        grid=(count, rows // tile),
        in_specs=[
            pl.BlockSpec(memory_space=pltpu.SMEM),
            pl.BlockSpec((1, 1, steps, tile, width), lambda s, i: (first + s, c, 0, i, 0)),
            pl.BlockSpec((1, steps, tile, width), lambda s, i: (s, 0, i, 0)),
        ],
        out_specs=[
            pl.BlockSpec((sets - 1, 1, 2, tile, width), lambda s, i: (0, s, 0, i, 0)),
            pl.BlockSpec((1, 2, tile, width), lambda s, i: (s, 0, i, 0)),
        ],
        out_shape=[
            jax.ShapeDtypeStruct((sets - 1, count, 2, rows, width), jnp.bfloat16),
            jax.ShapeDtypeStruct((count, 2, rows, width), jnp.float32),
        ],
        cost_estimate=pl.CostEstimate(
            flops=count * rows * width * 8 * steps * sets,
            bytes_accessed=count * rows * width * 28,
            transcendentals=0,
        ),
    )(weights, fields, mate)


def project_kernel(mine_ref, got_ref, q_ref, p_ref, out_ref, total):
    s = pl.program_id(0)

    def whole(k):
        value = mine_ref[0, k]
        for d in range(got_ref.shape[0]):
            value = value + got_ref[d, 0, k].astype(jnp.float32)
        return value.astype(jnp.bfloat16)

    def dot(left, right):
        return jnp.dot(left, right, preferred_element_type=jnp.float32)

    real, imag = whole(0), whole(1)
    image_real = (dot(real, q_ref[0, 0, 0]) - dot(imag, q_ref[0, 0, 1])).astype(jnp.bfloat16)
    image_imag = (dot(real, q_ref[0, 0, 1]) + dot(imag, q_ref[0, 0, 0])).astype(jnp.bfloat16)
    far = dot(p_ref[0, 0], image_real) + dot(p_ref[0, 1], image_imag)

    @pl.when(s == 0)
    def _():
        total[...] = far

    @pl.when(s > 0)
    def _():
        total[...] += far

    @pl.when(s == pl.num_programs(0) - 1)
    def _():
        out_ref[...] = total[...].astype(out_ref.dtype)


def project(mine, got, columns, turned, g):
    faces, _, rows, width = mine.shape
    angles = columns.shape[-1]
    tall = turned.shape[2]
    return pl.pallas_call(
        project_kernel,
        grid=(faces,),
        in_specs=[
            pl.BlockSpec((1, 2, rows, width), lambda s: (s, 0, 0, 0)),
            pl.BlockSpec((got.shape[0], 1, 2, rows, width), lambda s: (0, s, 0, 0, 0)),
            pl.BlockSpec((1, 1, 2, width, angles), lambda s: (g, s, 0, 0, 0)),
            pl.BlockSpec((1, 2, tall, rows), lambda s: (s, 0, 0, 0)),
        ],
        out_specs=pl.BlockSpec((tall, angles), lambda s: (0, 0)),
        out_shape=jax.ShapeDtypeStruct((tall, angles), jnp.bfloat16),
        scratch_shapes=[pltpu.VMEM((tall, angles), jnp.float32)],
        cost_estimate=pl.CostEstimate(
            flops=faces * rows * angles * (8 * width + 4 * tall),
            bytes_accessed=mine.size * 6 + columns.size * 2 + tall * angles * 2,
            transcendentals=0,
        ),
    )(mine, got, columns, turned)


def on_device(fields, step_index, omegas, col_phase, row_phase):
    n = lax.axis_size("freq")
    strips = lax.axis_size("strip")
    me = lax.axis_index("freq")
    faces, comps, steps = fields.shape[:3]
    freq_local, rows, angles = col_phase.shape[0], row_phase.shape[3], row_phase.shape[4]
    mate_id = me + 1 - 2 * lax.rem(me, 2)
    swap = [(i, i ^ 1) for i in range(n)]
    hops = range(2, n, 2)

    chunks = [(0, s, 1) for s in range(faces)] + [(c, 0, faces) for c in range(1, comps)]
    mates = []
    source = fields
    for c, first, count in chunks:
        if len(mates) >= 2:
            source, mates[-2] = lax.optimization_barrier((source, mates[-2]))
        piece = source[first : first + count, c]
        source, piece = lax.optimization_barrier((source, piece))
        mates.append(lax.ppermute(piece, "freq", swap))

    columns = lax.all_gather(col_phase, "strip", axis=3, tiled=True)

    indices = jnp.concatenate(
        [
            lax.dynamic_slice_in_dim(step_index, me * steps, steps),
            lax.dynamic_slice_in_dim(step_index, mate_id * steps, steps),
        ]
    ).astype(jnp.float32)

    def weights(g):
        devices = jnp.stack([lax.rem(me + d, n) for d in hops] + [me])
        phase = omegas[devices * freq_local + g][:, None] * indices[None, :]
        return jnp.stack([jnp.cos(phase), -jnp.sin(phase)], 1).reshape(-1, 2 * steps)

    all_weights = [weights(g) for g in range(freq_local)]
    mine, got = {}, {}
    for (c, first, count), mate in zip(chunks, mates):
        for g in range(freq_local):
            part, own = time_sums(all_weights[g], fields, mate, c, first, count)
            all_weights, own = lax.optimization_barrier((all_weights, own))
            mine.setdefault((c, g), []).append(own)
            moved = [
                lax.ppermute(part[k], "freq", [(i, (i + d) % n) for i in range(n)])
                for k, d in enumerate(hops)
            ]
            got.setdefault((c, g), []).append(jnp.stack(moved))

    row_phase, _ = lax.optimization_barrier((row_phase, mine[comps - 1, 0][-1]))

    def turned(g):
        p_real = row_phase[g, :, 0].reshape(faces, rows, strips, angles // strips)
        p_imag = row_phase[g, :, 1].reshape(faces, rows, strips, angles // strips)
        from_real = jnp.stack([p_real, p_imag], 3)
        from_imag = jnp.stack([-p_imag, p_real], 3)
        both = jnp.stack([from_real, from_imag], 1).reshape(faces, 2, rows, 2 * angles)
        return both.transpose(0, 1, 3, 2)

    turned_rows = [turned(g) for g in range(freq_local)]
    outs = []
    for c in range(comps):
        per_freq = []
        for g in range(freq_local):
            own, arrived = mine[c, g], got[c, g]
            own = own[0] if len(own) == 1 else jnp.concatenate(own, 0)
            arrived = arrived[0] if len(arrived) == 1 else jnp.concatenate(arrived, 1)
            far = project(own, arrived, columns, turned_rows[g], g)
            far = lax.all_to_all(far, "strip", split_axis=0, concat_axis=0, tiled=True)
            far = far.reshape(strips, 2, angles // strips, -1).astype(jnp.float32).sum(0)
            per_freq.append(far.transpose(1, 0, 2))
        outs.append(jnp.stack(per_freq, 1))
    return jnp.stack(outs, 3)


def solution(mesh):
    placed = (
        P(None, None, "freq", "strip", None),
        P(),
        P(),
        P("freq", None, None, "strip", None),
        P("freq", None, None, "strip", None),
    )
    return jax.shard_map(
        on_device,
        mesh=mesh,
        in_specs=placed,
        out_specs=P("strip", "freq", None, None, None),
        check_vma=False,
    )
```

```python
import functools

import jax
import jax.numpy as jnp
from jax import lax
from jax.experimental import pallas as pl
from jax.experimental.pallas import tpu as pltpu
from jax.sharding import PartitionSpec as P


def row_tile(rows, want):
    return want if rows % want == 0 else rows


def time_sums_kernel(sets, w_ref, own_ref, mate_ref, part_ref, mine_ref):
    steps, rows, width = own_ref.shape[2:]
    sub = row_tile(rows, 16)
    lane = row_tile(width, 256)

    def body(i, carry):
        r = pl.ds(pl.multiple_of(i * sub, sub), sub)
        for l in range(width // lane):
            cols = pl.ds(l * lane, lane)
            sums = [None] * (2 * sets)
            for t in range(2 * steps):
                raw = own_ref[0, 0, t, r, cols] if t < steps else mate_ref[0, t - steps, r, cols]
                record = raw.astype(jnp.float32)
                for k in range(2 * sets):
                    term = w_ref[k, t] * record
                    sums[k] = term if t == 0 else sums[k] + term
            for k in range(2 * (sets - 1)):
                part_ref[k // 2, 0, k % 2, r, cols] = sums[k].astype(jnp.bfloat16)
            for k in range(2):
                mine_ref[0, k, r, cols] = sums[2 * (sets - 1) + k]
        return carry

    lax.fori_loop(0, rows // sub, body, 0)


def time_sums(weights, fields, mate, c, first, count):
    steps, rows, width = fields.shape[2:]
    sets = weights.shape[0] // 2
    tile = row_tile(rows, 96)
    return pl.pallas_call(
        functools.partial(time_sums_kernel, sets),
        grid=(count, rows // tile),
        in_specs=[
            pl.BlockSpec(memory_space=pltpu.SMEM),
            pl.BlockSpec((1, 1, steps, tile, width), lambda s, i: (first + s, c, 0, i, 0)),
            pl.BlockSpec((1, steps, tile, width), lambda s, i: (s, 0, i, 0)),
        ],
        out_specs=[
            pl.BlockSpec((sets - 1, 1, 2, tile, width), lambda s, i: (0, s, 0, i, 0)),
            pl.BlockSpec((1, 2, tile, width), lambda s, i: (s, 0, i, 0)),
        ],
        out_shape=[
            jax.ShapeDtypeStruct((sets - 1, count, 2, rows, width), jnp.bfloat16),
            jax.ShapeDtypeStruct((count, 2, rows, width), jnp.float32),
        ],
        cost_estimate=pl.CostEstimate(
            flops=count * rows * width * 8 * steps * sets,
            bytes_accessed=count * rows * width * 28,
            transcendentals=0,
        ),
    )(weights, fields, mate)


def project_kernel(mine_ref, got_ref, q_ref, p_ref, out_ref, total):
    s = pl.program_id(0)

    def whole(k):
        value = mine_ref[0, k]
        for d in range(got_ref.shape[0]):
            value = value + got_ref[d, 0, k].astype(jnp.float32)
        return value.astype(jnp.bfloat16)

    def dot(left, right):
        return jnp.dot(left, right, preferred_element_type=jnp.float32)

    real, imag = whole(0), whole(1)
    image_real = (dot(real, q_ref[0, 0, 0]) - dot(imag, q_ref[0, 0, 1])).astype(jnp.bfloat16)
    image_imag = (dot(real, q_ref[0, 0, 1]) + dot(imag, q_ref[0, 0, 0])).astype(jnp.bfloat16)
    far = dot(p_ref[0, 0], image_real) + dot(p_ref[0, 1], image_imag)

    @pl.when(s == 0)
    def _():
        total[...] = far

    @pl.when(s > 0)
    def _():
        total[...] += far

    @pl.when(s == pl.num_programs(0) - 1)
    def _():
        out_ref[...] = total[...].astype(out_ref.dtype)


def project(mine, got, columns, turned, g):
    faces, _, rows, width = mine.shape
    angles = columns.shape[-1]
    tall = turned.shape[2]
    return pl.pallas_call(
        project_kernel,
        grid=(faces,),
        in_specs=[
            pl.BlockSpec((1, 2, rows, width), lambda s: (s, 0, 0, 0)),
            pl.BlockSpec((got.shape[0], 1, 2, rows, width), lambda s: (0, s, 0, 0, 0)),
            pl.BlockSpec((1, 1, 2, width, angles), lambda s: (g, s, 0, 0, 0)),
            pl.BlockSpec((1, 2, tall, rows), lambda s: (s, 0, 0, 0)),
        ],
        out_specs=pl.BlockSpec((tall, angles), lambda s: (0, 0)),
        out_shape=jax.ShapeDtypeStruct((tall, angles), jnp.bfloat16),
        scratch_shapes=[pltpu.VMEM((tall, angles), jnp.float32)],
        cost_estimate=pl.CostEstimate(
            flops=faces * rows * angles * (8 * width + 4 * tall),
            bytes_accessed=mine.size * 6 + columns.size * 2 + tall * angles * 2,
            transcendentals=0,
        ),
    )(mine, got, columns, turned)


def on_device(fields, step_index, omegas, col_phase, row_phase):
    n = lax.axis_size("freq")
    strips = lax.axis_size("strip")
    me = lax.axis_index("freq")
    faces, comps, steps = fields.shape[:3]
    freq_local, rows, angles = col_phase.shape[0], row_phase.shape[3], row_phase.shape[4]
    mate_id = me + 1 - 2 * lax.rem(me, 2)
    swap = [(i, i ^ 1) for i in range(n)]
    hops = range(2, n, 2)

    chunks = [(0, s, 1) for s in range(faces)] + [(c, 0, faces) for c in range(1, comps)]
    columns = lax.all_gather(col_phase, "strip", axis=3, tiled=True)

    indices = jnp.concatenate(
        [
            lax.dynamic_slice_in_dim(step_index, me * steps, steps),
            lax.dynamic_slice_in_dim(step_index, mate_id * steps, steps),
        ]
    ).astype(jnp.float32)

    def weights(g):
        devices = jnp.stack([lax.rem(me + d, n) for d in hops] + [me])
        phase = omegas[devices * freq_local + g][:, None] * indices[None, :]
        return jnp.stack([jnp.cos(phase), -jnp.sin(phase)], 1).reshape(-1, 2 * steps)

    all_weights = [weights(g) for g in range(freq_local)]
    mine, got = {}, {}
    source, mates = fields, []

    def swap_next():
        nonlocal source
        if len(mates) < len(chunks):
            c, first, count = chunks[len(mates)]
            piece = source[first : first + count, c]
            source, piece = lax.optimization_barrier((source, piece))
            mates.append(lax.ppermute(piece, "freq", swap))

    swap_next()
    swap_next()
    for k, (c, first, count) in enumerate(chunks):
        for g in range(freq_local):
            part, own = time_sums(all_weights[g], fields, mates[k], c, first, count)
            all_weights, source, own = lax.optimization_barrier((all_weights, source, own))
            moved = [
                lax.ppermute(part[j], "freq", [(i, (i + d) % n) for i in range(n)])
                for j, d in enumerate(hops)
            ]
            mine.setdefault((c, g), []).append(own)
            got.setdefault((c, g), []).append(jnp.stack(moved))
        swap_next()

    row_phase, _ = lax.optimization_barrier((row_phase, mine[comps - 1, 0][-1]))

    def turned(g):
        p_real = row_phase[g, :, 0].reshape(faces, rows, strips, angles // strips)
        p_imag = row_phase[g, :, 1].reshape(faces, rows, strips, angles // strips)
        from_real = jnp.stack([p_real, p_imag], 3)
        from_imag = jnp.stack([-p_imag, p_real], 3)
        both = jnp.stack([from_real, from_imag], 1).reshape(faces, 2, rows, 2 * angles)
        return both.transpose(0, 1, 3, 2)

    turned_rows = [turned(g) for g in range(freq_local)]
    outs = []
    for c in range(comps):
        per_freq = []
        for g in range(freq_local):
            own, arrived = mine[c, g], got[c, g]
            own = own[0] if len(own) == 1 else jnp.concatenate(own, 0)
            arrived = arrived[0] if len(arrived) == 1 else jnp.concatenate(arrived, 1)
            far = project(own, arrived, columns, turned_rows[g], g)
            far = lax.all_to_all(far, "strip", split_axis=0, concat_axis=0, tiled=True)
            far = far.reshape(strips, 2, angles // strips, -1).astype(jnp.float32).sum(0)
            per_freq.append(far.transpose(1, 0, 2))
        outs.append(jnp.stack(per_freq, 1))
    return jnp.stack(outs, 3)


def solution(mesh):
    placed = (
        P(None, None, "freq", "strip", None),
        P(),
        P(),
        P("freq", None, None, "strip", None),
        P("freq", None, None, "strip", None),
    )
    return jax.shard_map(
        on_device,
        mesh=mesh,
        in_specs=placed,
        out_specs=P("strip", "freq", None, None, None),
        check_vma=False,
    )
```
